128 devices in a mesh: tiles: 128 (over z, x, y, core).
Axes of the slice: x: 4, y: 4, z: 4, core: 2. Of those that a mesh axis runs over, the one named last changes fastest.
Arguments:
- fields: bfloat16 [128, 64, 64, 128], P('tiles')
- cotangent: bfloat16 [128, 64, 64, 128], P('tiles'), may hold values from -6 to 6
- ocean_mask: int32 [128, 64, 64], P('tiles'), may hold values from 0 to 1
- neighbours: int32 [128, 8], P('tiles'), may hold values from -1 to 127, as said below
- kernel: float32 [7, 7, 128], replicated, may hold values from -0.875 to 0.875
- conv_bias: float32 [128], replicated, may hold values from -0.5 to 0.5
- ln_gain: float32 [128], replicated, may hold values from 0.5 to 1.5
- ln_bias: float32 [128], replicated, may hold values from -1.5 to 1.5
- weight_in: bfloat16 [128, 512], replicated, may hold values from -0.5 to 0.5
- bias_in: float32 [512], replicated, may hold values from -1.5 to 1.5
- weight_out: bfloat16 [512, 128], replicated, may hold values from -0.25 to 0.25
- bias_out: float32 [128], replicated, may hold values from -1.5 to 1.5
- layer_scale: float32 [128], replicated, may hold values from 0.3 to 1.5
Outputs:
- updated: bfloat16 [128, 64, 64, 128], P('tiles')
- d_fields: float32 [128, 64, 64, 128], P('tiles')
- d_kernel: float32 [7, 7, 128], replicated
- d_conv_bias: float32 [128], replicated
- d_ln_gain: float32 [128], replicated
- d_ln_bias: float32 [128], replicated
- d_weight_in: float32 [128, 512], replicated
- d_bias_in: float32 [512], replicated
- d_weight_out: float32 [512, 128], replicated
- d_bias_out: float32 [128], replicated
- d_layer_scale: float32 [128], replicated
The draws below stay inside these ranges and needn't reach their ends.
Inputs may be any that keep to these rules, and one draw needn't show every extreme that they name: `neighbours`: entries name tiles across the north, south, west, east, north-west, north-east, south-west and south-east sides; the lists are mutual (a tile lists its neighbour on one side and is listed on the opposite one) and follow one grid of tiles (where a tile and its listed neighbour both list a tile, it is the one the grid places there; a tile listed by nobody around it holds no ocean). Every listed tile is held by a device at most 7 indices away along tiles, and some listed tile is exactly 7 away; the index offset of a given side is not the same for all tiles.
All inputs are finite; a program needn't handle non-finite values.
Results may differ from the reference program's by a relative error of at most 0.0062.
Values may be sent and summed in bfloat16 or wider, within the bound.
A program may use at most 448 MiB of HBM per device.

```python
import math
import jax
import jax.numpy as jnp
from jax import lax

TPD = 1
TILE = 64
C = 128
F = 512
KSIZE = 7
BAND = 4
TILES = 128


def tile_layout(key):
    live_key, order_key = jax.random.split(jax.random.fold_in(key, 7))
    position = jnp.arange(TILES, dtype=jnp.int32)
    grid_row = position // BAND
    grid_col = position % BAND
    grid_rows = TILES // BAND
    first_row = max(TPD // BAND - 1, 0)
    live_tile = jax.random.randint(live_key, (TILES,), 0, 4) > 0
    live_tile = live_tile | (grid_row < 2) | (grid_row >= grid_rows - 2)
    live_tile = live_tile | (grid_row == first_row) | (grid_row == first_row + 1)
    live_tile = live_tile | (position // TPD == TILES // TPD // 2)
    scores = jax.random.randint(order_key, (grid_rows, BAND), 0, 1 << 20) * BAND + jnp.arange(BAND, dtype=jnp.int32)[None, :]
    scores = scores.at[first_row, 0].set(-1)
    scores = scores.at[first_row + 1, 1].set(1 << 23)
    ordering = jnp.argsort(scores, axis=1)
    ranking = jnp.argsort(ordering, axis=1).astype(jnp.int32)
    tile_slot = grid_row * BAND + ranking.reshape(-1)
    return (live_tile, grid_row, grid_col, tile_slot)


def draw_neighbours(key, part):
    live_tile, grid_row, grid_col, tile_slot = tile_layout(key)
    step_row = jnp.array([-1, 1, 0, 0, -1, -1, 1, 1], jnp.int32)
    step_col = jnp.array([0, 0, -1, 1, -1, 1, -1, 1], jnp.int32)
    target_row = grid_row[:, None] + step_row[None, :]
    target_col = grid_col[:, None] + step_col[None, :]
    inside = (target_row >= 0) & (target_row < TILES // BAND) & (target_col >= 0) & (target_col < BAND)
    target = jnp.where(inside, target_row * BAND + target_col, 0)
    usable = inside & live_tile[target] & live_tile[:, None]
    listing = jnp.where(usable, tile_slot[target], -1).astype(jnp.int32)
    return jnp.zeros((TILES, 8), jnp.int32).at[tile_slot].set(listing)


def draw_ocean_mask(key, part):
    live_tile, grid_row, grid_col, tile_slot = tile_layout(key)
    pixels = jax.random.randint(jax.random.fold_in(key, 11), (TILES, TILE, TILE), 0, 20) < 17
    by_position = (pixels & live_tile[:, None, None]).astype(jnp.int32)
    return jnp.zeros((TILES, TILE, TILE), jnp.int32).at[tile_slot].set(by_position)


def draw_fields(key, part):
    base_key, chan_key, pixel_key = jax.random.split(key, 3)
    base = jnp.clip(jax.random.normal(base_key, (TILES, TILE, TILE, C), jnp.float32), -6.0, 6.0)
    chan_scale = jnp.exp(jax.random.uniform(chan_key, (TILES, 1, 1, C), jnp.float32, -1.15, 1.15))
    pixel_scale = jnp.exp(jax.random.uniform(pixel_key, (TILES, TILE, TILE, 1), jnp.float32, -0.7, 0.7))
    return (base * chan_scale * pixel_scale).astype(jnp.bfloat16)


def block_scale(own_key, dims, cuts, low, largest):
    def one(axis_at, blocks):
        steps = jax.random.uniform(jax.random.fold_in(jax.random.fold_in(own_key, 6), axis_at), (blocks,), jnp.float32, low / len(cuts), largest / len(cuts))
        return jnp.repeat(jnp.exp(steps), dims[axis_at] // blocks).reshape((-1,) + (1,) * (len(dims) - axis_at - 1))

    factor_of = one(*cuts[0])
    for cut in cuts[1:]:
        factor_of = factor_of * one(*cut)
    return factor_of


def bell_draw(own_key, shape, scale, most, pieces=(), held_as=jnp.bfloat16):
    values = jax.random.normal(own_key, shape, jnp.float32) * scale
    if len(pieces) > 0:
        values = block_scale(own_key, shape, pieces, -0.22, 0.18) * values
    return jnp.clip(values, min=-most, max=most).astype(held_as)


def setup_inputs(seed: int = 0) -> dict:
    keys = jax.random.split(jax.random.key(seed), 14)
    return {
        "fields": draw_fields(jax.random.fold_in(keys[13], 71), 0),
        "cotangent": bell_draw(keys[1], (TILES, TILE, TILE, C), 1.0, 6.0, ((0, 128),)),
        "ocean_mask": draw_ocean_mask(jax.random.fold_in(keys[13], 71), 0),
        "neighbours": draw_neighbours(jax.random.fold_in(keys[13], 71), 0),
        "kernel": bell_draw(keys[4], (KSIZE, KSIZE, C), (KSIZE * KSIZE) ** -0.5, 0.875, (), jnp.float32),
        "conv_bias": jnp.clip(jax.random.uniform(keys[5], (C,), jnp.float32, -0.5, 0.5), -0.5, 0.5),
        "ln_gain": jnp.clip(1.0 + 0.1 * jax.random.normal(keys[6], (C,), jnp.float32), 0.5, 1.5),
        "ln_bias": bell_draw(keys[7], (C,), 0.3, 1.5, (), jnp.float32),
        "weight_in": bell_draw(keys[8], (C, F), C ** -0.5, 0.5),
        "bias_in": bell_draw(keys[9], (F,), 0.3, 1.5, (), jnp.float32),
        "weight_out": bell_draw(keys[10], (F, C), F ** -0.5, 0.25),
        "bias_out": bell_draw(keys[11], (C,), 0.3, 1.5, (), jnp.float32),
        "layer_scale": jnp.clip(jnp.exp(jax.random.uniform(keys[12], (C,), jnp.float32, math.log(0.3), math.log(1.5))), 0.3, 1.5),
    }


EPS = 1e-06
GELU_K = 0.7978845608028654
GELU_C = 0.044715
CONTRACT_LAST = (((1,), (1,)), ((), ()))
CONTRACT_ROWS = (((0,), (0,)), ((), ()))

def gelu_parts(hidden):
    cube = hidden * hidden * hidden
    tanh_part = jnp.tanh(GELU_K * (hidden + GELU_C * cube))
    gelu_value = 0.5 * hidden * (1.0 + tanh_part)
    gelu_slope = 0.5 * (1.0 + tanh_part) + 0.5 * hidden * (1.0 - tanh_part * tanh_part) * GELU_K * (1.0 + 3.0 * GELU_C * hidden * hidden)
    return (gelu_value, gelu_slope)

def block_core(conv, signal, ln_gain, ln_bias, weight_in, bias_in, weight_out, bias_out, layer_scale):
    mean_part = lax.optimization_barrier(jnp.mean(conv, axis=-1, keepdims=True))
    centred = conv - mean_part
    inv_std = lax.rsqrt(lax.optimization_barrier(jnp.mean(centred * centred, axis=-1, keepdims=True)) + EPS)
    normed = centred * inv_std
    lifted = (normed * ln_gain + ln_bias).astype(jnp.bfloat16)
    hidden = jnp.dot(lifted, weight_in, preferred_element_type=jnp.float32) + bias_in
    gelu_value, gelu_slope = gelu_parts(hidden)
    activated = gelu_value.astype(jnp.bfloat16)
    branch = jnp.dot(activated, weight_out, preferred_element_type=jnp.float32) + bias_out
    d_branch = signal * layer_scale
    branch_low = d_branch.astype(jnp.bfloat16)
    d_activated = lax.dot_general(branch_low, weight_out, CONTRACT_LAST, preferred_element_type=jnp.float32)
    d_hidden = d_activated * gelu_slope
    hidden_low = d_hidden.astype(jnp.bfloat16)
    d_lifted = lax.dot_general(hidden_low, weight_in, CONTRACT_LAST, preferred_element_type=jnp.float32)
    d_normed = d_lifted * ln_gain
    d_conv = inv_std * (d_normed - lax.optimization_barrier(jnp.mean(d_normed, axis=-1, keepdims=True)) - normed * lax.optimization_barrier(jnp.mean(d_normed * normed, axis=-1, keepdims=True)))
    partials = (lax.optimization_barrier(jnp.sum(signal * branch, axis=0)), lax.optimization_barrier(jnp.sum(d_branch, axis=0)), lax.dot_general(activated, branch_low, CONTRACT_ROWS, preferred_element_type=jnp.float32), lax.optimization_barrier(jnp.sum(d_hidden, axis=0)), lax.dot_general(lifted, hidden_low, CONTRACT_ROWS, preferred_element_type=jnp.float32), lax.optimization_barrier(jnp.sum(d_lifted * normed, axis=0)), lax.optimization_barrier(jnp.sum(d_lifted, axis=0)))
    return (branch, d_conv, partials)

def frame_strips(stack, radius):
    extent = stack.shape[1]
    top_rows = stack[:, :radius]
    bottom_rows = stack[:, extent - radius:]
    left_cols = jnp.swapaxes(stack[:, :, :radius], 1, 2)
    right_cols = jnp.swapaxes(stack[:, :, extent - radius:], 1, 2)
    return jnp.stack([top_rows, bottom_rows, left_cols, right_cols], axis=1)

def assemble(middle, picked, radius):
    extent = middle.shape[1]
    top_mid = picked[:, 0, 1]
    bottom_mid = picked[:, 1, 0]
    left_mid = jnp.swapaxes(picked[:, 2, 3], 1, 2)
    right_mid = jnp.swapaxes(picked[:, 3, 2], 1, 2)
    north_west = picked[:, 4, 1, :, extent - radius:]
    north_east = picked[:, 5, 1, :, :radius]
    south_west = picked[:, 6, 0, :, extent - radius:]
    south_east = picked[:, 7, 0, :, :radius]
    upper = jnp.concatenate([north_west, top_mid, north_east], axis=2)
    centre_band = jnp.concatenate([left_mid, middle, right_mid], axis=2)
    lower = jnp.concatenate([south_west, bottom_mid, south_east], axis=2)
    return jnp.concatenate([upper, centre_band, lower], axis=1)

def depthwise(padded, kernel):
    ksize = kernel.shape[0]
    out_size = padded.shape[1] - ksize + 1
    total = jnp.zeros((padded.shape[0], out_size, out_size, padded.shape[3]), jnp.float32)
    for row_tap in range(ksize):
        for col_tap in range(ksize):
            total = total + padded[:, row_tap:row_tap + out_size, col_tap:col_tap + out_size, :] * kernel[row_tap, col_tap]
    return total

def kernel_grad(padded, d_conv, ksize):
    out_size = d_conv.shape[1]
    rows_list = []
    for row_tap in range(ksize):
        cols_list = []
        for col_tap in range(ksize):
            window = padded[:, row_tap:row_tap + out_size, col_tap:col_tap + out_size, :]
            cols_list.append(lax.optimization_barrier(jnp.sum(window * d_conv, axis=(0, 1, 2))))
        rows_list.append(jnp.stack(cols_list))
    return jnp.stack(rows_list)

def reference(fields, cotangent, ocean_mask, neighbours, kernel, conv_bias, ln_gain, ln_bias, weight_in, bias_in, weight_out, bias_out, layer_scale):
    radius = KSIZE // 2
    mask_float = ocean_mask.astype(jnp.float32)[..., None]
    masked = (fields.astype(jnp.float32) * mask_float).astype(jnp.bfloat16)
    listed = neighbours >= 0
    safe_ids = jnp.where(listed, neighbours, 0).astype(jnp.int32)
    strips = frame_strips(masked, radius)

    def pick(table, tile_index):
        chosen = jnp.take(table, safe_ids[tile_index], axis=0)
        keep = listed[tile_index][:, None, None, None, None]
        return jnp.where(keep, chosen, jnp.zeros_like(chosen))[None]

    def one_tile(table, tile_index):
        return lax.dynamic_slice_in_dim(table, tile_index, 1, 0)

    def forward_tile(carry, tile_index):
        middle = one_tile(masked, tile_index)
        padded = assemble(middle, pick(strips, tile_index), radius).astype(jnp.float32)
        conv = depthwise(padded, kernel) + conv_bias
        tile_mask = one_tile(mask_float, tile_index)
        signal = one_tile(cotangent, tile_index).astype(jnp.float32) * tile_mask
        branch, d_conv, partials = block_core(conv.reshape(-1, C), signal.reshape(-1, C), ln_gain, ln_bias, weight_in, bias_in, weight_out, bias_out, layer_scale)
        branch = branch.reshape(conv.shape)
        d_conv = d_conv.reshape(conv.shape)
        updated = (tile_mask * (middle.astype(jnp.float32) + layer_scale * branch)).astype(jnp.bfloat16)
        partials = partials + (kernel_grad(padded, d_conv, KSIZE), lax.optimization_barrier(jnp.sum(d_conv, axis=(0, 1, 2))))
        carry = tuple((running + piece_sum for running, piece_sum in zip(carry, partials)))
        return (carry, (updated[0], d_conv[0]))
    start = (jnp.zeros((C,), jnp.float32), jnp.zeros((C,), jnp.float32), jnp.zeros((F, C), jnp.float32), jnp.zeros((F,), jnp.float32), jnp.zeros((C, F), jnp.float32), jnp.zeros((C,), jnp.float32), jnp.zeros((C,), jnp.float32), jnp.zeros((KSIZE, KSIZE, C), jnp.float32), jnp.zeros((C,), jnp.float32))
    tile_order = jnp.arange(TILES, dtype=jnp.int32)
    totals, outputs = lax.scan(forward_tile, start, tile_order)
    updated, d_conv_all = outputs
    d_strips = frame_strips(d_conv_all, radius)
    flipped = kernel[::-1, ::-1]

    def backward_tile(tile_index):
        padded = assemble(one_tile(d_conv_all, tile_index), pick(d_strips, tile_index), radius)
        back = depthwise(padded, flipped)
        tile_mask = one_tile(mask_float, tile_index)
        signal = one_tile(cotangent, tile_index).astype(jnp.float32) * tile_mask
        return (tile_mask * (signal + back))[0]
    d_fields = lax.map(backward_tile, tile_order)
    grad_scale = 1.0 / math.sqrt(TILES * TILE * TILE)
    scaled = [running * grad_scale for running in totals]
    return (updated, d_fields, scaled[7], scaled[8], scaled[5], scaled[6], scaled[4], scaled[3], scaled[2], scaled[1], scaled[0])
```

```python
import functools
import math

import jax
import jax.numpy as jnp
from jax import lax
from jax.experimental import pallas as pl
from jax.experimental.pallas import tpu as pltpu
from jax.sharding import PartitionSpec as P

REACH = 7
OFFS = [o for o in range(-REACH, REACH + 1) if o != 0]
NOFF = len(OFFS)
EPS = 1e-06
GELU_K = 0.7978845608028654
GELU_C = 0.044715
MESH = pl.DeviceIdType.MESH
BF = jnp.bfloat16
F32 = jnp.float32
TS = 64
CH = 128
R = 3
NS = 8
NQ = 8
HG = 16
NP = NQ + 6
STRIP_OF_SIDE = (0, 1, 2, 3, 0, 0, 1, 1)
VMEM_LIMIT = 60 << 20


def vspec():
    return pl.BlockSpec(memory_space=pltpu.VMEM)


def sspec():
    return pl.BlockSpec(memory_space=pltpu.SMEM)


def strip_index(nb_ref, me, off):
    idx = jnp.int32(0)
    for side in range(8):
        idx = jnp.where(nb_ref[0, side] == me + off, STRIP_OF_SIDE[side], idx)
    return idx


def recv_slot(nb_ref, me, side):
    nb = nb_ref[0, side]
    off = nb - me
    slot = jnp.where(off < 0, off + REACH, off + REACH - 1)
    listed = nb >= 0
    return jnp.where(listed, slot, 0), jnp.where(listed, 1.0, 0.0).astype(F32)


def plane_matrix(permuted):
    row = lax.broadcasted_iota(jnp.int32, (NP * NS, CH), 0)
    lane = lax.broadcasted_iota(jnp.int32, (NP * NS, CH), 1)
    col = NQ * (row % NS) + row // NS - R
    inner = (col % NQ) * NS + col // NQ if permuted else col
    target = jnp.where(col < 0, TS + R + col, jnp.where(col >= TS, col + R, inner))
    return jnp.where(lane == target, 1.0, 0.0).astype(F32)


def unpermute_matrix(rows):
    n = TS * rows
    row = lax.broadcasted_iota(jnp.int32, (n, n), 0)
    lane = lax.broadcasted_iota(jnp.int32, (n, n), 1)
    col = row % TS
    target = (row // TS) * TS + (col % NQ) * NS + col // NQ
    return jnp.where(lane == target, 1.0, 0.0)


def dot(a, b):
    return jnp.dot(a, b, preferred_element_type=F32)


def write_pieces(nb_ref, me, strips, out):
    for k, off in enumerate(OFFS):
        out[k] = strips[strip_index(nb_ref, me, off)]


def pack_kernel(nb_ref, me_ref, top, bottom, left, right, mnat, mtr, out, strips, cols):
    me = me_ref[0]
    eye = jnp.where(
        lax.broadcasted_iota(jnp.int32, (TS, TS), 0) == lax.broadcasted_iota(jnp.int32, (TS, TS), 1),
        1.0,
        0.0,
    ).astype(F32)

    def masked(mask_row, value):
        return dot((eye * mask_row[:, :TS]).astype(BF), value).astype(BF)

    for w in range(R):
        strips[0, w] = masked(mnat[w], top[w])
        strips[1, w] = masked(mnat[TS - R + w], bottom[w + 1])
    for which, block, first in ((2, left, 0), (3, right, HG - R)):
        cols[...] = block[...].astype(F32).reshape(TS * HG, CH)
        for w in range(R):
            value = cols[pl.ds(first + w, TS, stride=HG), :].astype(BF)
            column = w if which == 2 else TS - R + w
            strips[which, w] = masked(mtr[column], value)
    write_pieces(nb_ref, me, strips, out)


def pack(nb, me, fields, mnat, mtr):
    n = fields.shape[0] // TS
    del n
    return pl.pallas_call(
        pack_kernel,
        grid=(1,),
        out_shape=jax.ShapeDtypeStruct((NOFF, R, TS, CH), BF),
        in_specs=[
            sspec(),
            sspec(),
            pl.BlockSpec((4, TS, CH), lambda i: (0, 0, 0)),
            pl.BlockSpec((4, TS, CH), lambda i: (TS // 4 - 1, 0, 0)),
            pl.BlockSpec((TS, HG, CH), lambda i: (0, 0, 0)),
            pl.BlockSpec((TS, HG, CH), lambda i: (0, TS // HG - 1, 0)),
            pl.BlockSpec((TS, 1, CH), lambda i: (0, 0, 0)),
            pl.BlockSpec((TS, 1, CH), lambda i: (0, 0, 0)),
        ],
        out_specs=pl.BlockSpec((NOFF, R, TS, CH), lambda i: (0, 0, 0, 0)),
        scratch_shapes=[pltpu.VMEM((4, R, TS, CH), BF), pltpu.VMEM((TS * HG, CH), F32)],
        compiler_params=pltpu.CompilerParams(vmem_limit_bytes=VMEM_LIMIT),
    )(nb, me, fields, fields, fields, fields, mnat, mtr)


def exchange_kernel(n, pieces, out, send_sem, recv_sem):
    me = lax.axis_index("tiles")
    barrier = pltpu.get_barrier_semaphore()
    for off in OFFS:
        pl.semaphore_signal(barrier, inc=1, device_id=(lax.rem(me + off + n, n),), device_id_type=MESH)
    pl.semaphore_wait(barrier, NOFF)
    copies = []
    for k, off in enumerate(OFFS):
        copies.append(
            pltpu.make_async_remote_copy(
                src_ref=pieces.at[k],
                dst_ref=out.at[NOFF - 1 - k],
                send_sem=send_sem.at[k],
                recv_sem=recv_sem.at[NOFF - 1 - k],
                device_id=(lax.rem(me + off + n, n),),
                device_id_type=MESH,
            )
        )
    order = sorted(range(NOFF), key=lambda k: -abs(OFFS[k]))
    for k in order:
        copies[k].start()
    for k in order:
        copies[k].wait()


def exchange(pieces, n, cid):
    return pl.pallas_call(
        functools.partial(exchange_kernel, n),
        out_shape=jax.ShapeDtypeStruct(pieces.shape, pieces.dtype),
        in_specs=[pl.BlockSpec(memory_space=pltpu.VMEM)],
        out_specs=pl.BlockSpec(memory_space=pltpu.VMEM),
        scratch_shapes=[pltpu.SemaphoreType.DMA((NOFF,)), pltpu.SemaphoreType.DMA((NOFF,))],
        compiler_params=pltpu.CompilerParams(
            collective_id=cid, has_side_effects=True, vmem_limit_bytes=VMEM_LIMIT
        ),
    )(pieces)


def place_halo_columns(nb_ref, me, recv, halo):
    halo[...] = jnp.zeros(halo.shape, F32)
    west, _ = recv_slot(nb_ref, me, 2)
    east, _ = recv_slot(nb_ref, me, 3)
    for w in range(R):
        halo[pl.ds(R * HG + w, TS, stride=HG), :] = recv[west, w].astype(F32)
        halo[pl.ds(R * HG + R + w, TS, stride=HG), :] = recv[east, w].astype(F32)
    for side, row0, col0 in ((4, 0, 0), (5, 0, R), (6, R + TS, 0), (7, R + TS, R)):
        slot, _ = recv_slot(nb_ref, me, side)
        first = TS - R if col0 == 0 else 0
        for w in range(R):
            at = (row0 + w) * HG + col0
            halo[at : at + R, :] = recv[slot, w].astype(F32)[first : first + R, :]


def flag_lanes(nb_ref, me, sides):
    lane = lax.broadcasted_iota(jnp.int32, (1, CH), 1)
    total = jnp.zeros((1, CH), F32)
    for side, low, high in zip(sides, (0, TS, TS + R), (TS, TS + R, TS + 2 * R)):
        if side is None:
            continue
        flag = recv_slot(nb_ref, me, side)[1]
        total = total + jnp.where((lane >= low) & (lane < high), flag, 0.0)
    return total


def fill_edge_rows(nb_ref, me, recv, halo, planes):
    matrix = plane_matrix(False)
    for sides, row0 in (((0, 4, 5), 0), ((1, 6, 7), R + TS)):
        flags = flag_lanes(nb_ref, me, sides)
        lhs = (matrix * flags).astype(BF)
        slot, _ = recv_slot(nb_ref, me, sides[0])
        for w in range(R):
            side_cols = halo[(row0 + w) * HG : (row0 + w + 1) * HG, :].astype(BF)
            rhs = jnp.concatenate([recv[slot, w], side_cols, jnp.zeros((48, CH), BF)], axis=0)
            planes[row0 + w] = dot(lhs, rhs)


def conv_row(planes, taps, i):
    acc = [None] * NQ
    for a in range(7):
        row = [planes[i + a, p * NS : (p + 1) * NS, :] for p in range(NP)]
        for b in range(7):
            tap = taps[a * 7 + b]
            for q in range(NQ):
                term = row[q + b] * tap
                acc[q] = term if acc[q] is None else acc[q] + term
    return jnp.concatenate(acc, axis=0)


def fold(value):
    return jnp.sum(value.reshape(-1, 8, value.shape[-1]), axis=0)


ROWS = 4
BLOCK = ROWS * TS
CONTRACT0 = (((0,), (0,)), ((), ()))


def core_kernel(
    nb_ref, me_ref, fields, cot, recv, mnat, mperm, kern, cbias, gain, beta, win, bin_, wout, bout, scale,
    updated, dconv, sig_out, pieces, gwi, gwot, small,
    planes, halo, taps, cv, df, wit, wot, strips, gbi, gsum,
):
    me = me_ref[0]
    place_halo_columns(nb_ref, me, recv, halo)
    for t in range(49):
        taps[t] = jnp.broadcast_to(kern[t], (NS, CH))
    wit[...] = win[...].T
    wot[...] = wout[...].T
    fill_edge_rows(nb_ref, me, recv, halo, planes)
    matrix = plane_matrix(False)
    flags = flag_lanes(nb_ref, me, (None, 2, 3))

    def prepare(i, carry):
        lhs = (matrix * (mnat[i] + flags)).astype(BF)
        side_cols = halo[pl.ds(pl.multiple_of((i + R) * HG, HG), HG), :].astype(BF)
        pad = jnp.zeros((48, CH), BF)
        left = jnp.concatenate([fields[i], side_cols, pad], axis=0)
        right = jnp.concatenate([cot[i], jnp.zeros((64, CH), BF)], axis=0)
        out = dot(lhs, jnp.concatenate([left, right], axis=1))
        planes[i + R] = out[:, :CH]
        sig_out[pl.ds(pl.multiple_of(i * TS, TS), TS), :] = out[R * NS : R * NS + TS, CH:].astype(BF)
        return carry

    lax.fori_loop(0, TS, prepare, 0)

    def convolve(i, carry):
        cv[pl.ds(pl.multiple_of(i * TS, TS), TS), :] = conv_row(planes, taps, i) + cbias[...]
        return carry

    lax.fori_loop(0, TS, convolve, 0)

    gwi[...] = jnp.zeros(gwi.shape, F32)
    gwot[...] = jnp.zeros(gwot.shape, F32)
    gbi[...] = jnp.zeros(gbi.shape, F32)
    gsum[...] = jnp.zeros(gsum.shape, F32)
    small[...] = jnp.zeros(small.shape, F32)
    ones = jnp.full((CH, CH), 1.0 / CH, BF)
    all_ones = jnp.full((8, BLOCK), 1.0, BF)
    ones2 = jnp.full((2 * CH, CH), 1.0 / CH, BF)
    back_matrix = unpermute_matrix(ROWS).astype(BF)

    def block(n, carry):
        rows = pl.ds(pl.multiple_of(n * BLOCK, BLOCK), BLOCK)
        x = cv[rows, :]
        x_high = x.astype(BF)
        x_low = (x - x_high.astype(F32)).astype(BF)
        centred = x - dot(jnp.concatenate([x_high, x_low], axis=1), ones2)
        inv = lax.rsqrt(dot((centred * centred).astype(BF), ones) + EPS)
        normed = centred * inv
        lifted = (normed * gain[...] + beta[...]).astype(BF)
        sig = sig_out[rows, :].astype(F32)
        d_branch = sig * scale[...]
        branch_low = d_branch.astype(BF)
        hidden = dot(lifted, win[...]) + bin_[...]
        d_act = dot(branch_low, wot[...])
        square = hidden * hidden
        half = 0.5 * hidden
        t = jnp.tanh(hidden * (GELU_K + (GELU_K * GELU_C) * square))
        up = 1.0 + t
        act = (half * up).astype(BF)
        slope = 0.5 * up + (half * (1.0 - t * t)) * (GELU_K + (3.0 * GELU_K * GELU_C) * square)
        d_hidden = d_act * slope
        hidden_low = d_hidden.astype(BF)
        branch = dot(act, wout[...]) + bout[...]
        d_lifted = dot(hidden_low, wit[...])
        gwot[...] += lax.dot_general(branch_low, act, CONTRACT0, preferred_element_type=F32)
        gwi[...] += lax.dot_general(lifted, hidden_low, CONTRACT0, preferred_element_type=F32)
        gbi[...] += dot(all_ones, hidden_low)
        e = d_lifted * gain[...]
        en = (e * normed).astype(BF)
        d_conv = inv * (e - dot(e.astype(BF), ones) - normed * dot(en, ones))
        gsum[0] += fold(d_conv)
        gsum[1] += fold(d_branch)
        df[rows, :] = d_conv
        dconv[rows, :] = d_conv.astype(BF)
        middle = jnp.concatenate(
            [planes[n * ROWS + R + w, R * NS : R * NS + TS, :] for w in range(ROWS)], axis=0
        )
        value = (middle + scale[...] * branch).astype(BF)
        natural = dot(back_matrix * mperm[n].astype(BF), value).astype(BF)
        updated[pl.ds(n * ROWS, ROWS)] = natural.reshape(ROWS, TS, CH)
        return carry

    lax.fori_loop(0, TS // ROWS, block, 0)

    one_row = unpermute_matrix(1).astype(BF)
    for w in range(R):
        strips[0, w] = dot(one_row, dconv[w * TS : (w + 1) * TS, :]).astype(BF)
        low = TS - R + w
        strips[1, w] = dot(one_row, dconv[low * TS : (low + 1) * TS, :]).astype(BF)
        for which, col in ((2, w), (3, TS - R + w)):
            first = (col % NQ) * NS + col // NQ
            strips[which, w] = df[pl.ds(first, TS, stride=TS), :].astype(BF)
    write_pieces(nb_ref, me, strips, pieces)

    for a in range(7):

        def gather(i, accs):
            accs = list(accs)
            row = [planes[i + a, p * NS : (p + 1) * NS, :] for p in range(NP)]
            first = pl.multiple_of(i * TS, TS)
            for q in range(NQ):
                grad = df[pl.ds(first + q * NS, NS), :]
                for b in range(7):
                    accs[b] = accs[b] + row[q + b] * grad
            return tuple(accs)

        accs = lax.fori_loop(0, TS, gather, tuple(jnp.zeros((8, CH), F32) for _ in range(7)))
        for b in range(7):
            small[a * 7 + b : a * 7 + b + 1, :] = jnp.sum(accs[b], axis=0, keepdims=True)
    small[49:50, :] = jnp.sum(gsum[0], axis=0, keepdims=True)
    small[50:51, :] = jnp.sum(gsum[1], axis=0, keepdims=True)
    for w in range(4):
        small[51 + w : 52 + w, :] = gbi[0:1, w * CH : (w + 1) * CH]


def core(nb, me, fields, cot, recv, mnat, mperm, kern, cbias, gain, beta, win, bin_, wout, bout, scale):
    hidden = win.shape[1]
    return pl.pallas_call(
        core_kernel,
        out_shape=(
            jax.ShapeDtypeStruct((TS, TS, CH), BF),
            jax.ShapeDtypeStruct((TS * TS, CH), BF),
            jax.ShapeDtypeStruct((TS * TS, CH), BF),
            jax.ShapeDtypeStruct((NOFF, R, TS, CH), BF),
            jax.ShapeDtypeStruct((CH, hidden), F32),
            jax.ShapeDtypeStruct((CH, hidden), F32),
            jax.ShapeDtypeStruct((64, CH), F32),
        ),
        in_specs=[sspec(), sspec()] + [vspec()] * 14,
        out_specs=(vspec(),) * 7,
        scratch_shapes=[
            pltpu.VMEM((TS + 2 * R, NP * NS, CH), F32),
            pltpu.VMEM(((TS + 2 * R) * HG, CH), F32),
            pltpu.VMEM((49, NS, CH), F32),
            pltpu.VMEM((TS * TS, CH), F32),
            pltpu.VMEM((TS * TS, CH), F32),
            pltpu.VMEM((hidden, CH), BF),
            pltpu.VMEM((CH, hidden), BF),
            pltpu.VMEM((4, R, TS, CH), BF),
            pltpu.VMEM((8, hidden), F32),
            pltpu.VMEM((2, 8, CH), F32),
        ],
        compiler_params=pltpu.CompilerParams(vmem_limit_bytes=VMEM_LIMIT),
    )(nb, me, fields, cot, recv, mnat, mperm, kern, cbias, gain, beta, win, bin_, wout, bout, scale)


def back_kernel(nb_ref, me_ref, recv, dconv, sig, mperm, kern, out, planes, halo, taps):
    me = me_ref[0]
    place_halo_columns(nb_ref, me, recv, halo)
    for t in range(49):
        taps[t] = jnp.broadcast_to(kern[48 - t], (NS, CH))
    fill_edge_rows(nb_ref, me, recv, halo, planes)
    lane = lax.broadcasted_iota(jnp.int32, (1, CH), 1)
    own = jnp.where(lane < TS, 1.0, 0.0)
    lhs = (plane_matrix(True) * (own + flag_lanes(nb_ref, me, (None, 2, 3)))).astype(BF)

    def prepare(i, carry):
        side_cols = halo[pl.ds(pl.multiple_of((i + R) * HG, HG), HG), :].astype(BF)
        mid = dconv[pl.ds(pl.multiple_of(i * TS, TS), TS), :]
        rhs = jnp.concatenate([mid, side_cols, jnp.zeros((48, CH), BF)], axis=0)
        planes[i + R] = dot(lhs, rhs)
        return carry

    lax.fori_loop(0, TS, prepare, 0)
    back_matrix = unpermute_matrix(ROWS).astype(BF)

    def convolve(n, carry):
        rows = pl.ds(pl.multiple_of(n * BLOCK, BLOCK), BLOCK)
        got = jnp.concatenate([conv_row(planes, taps, n * ROWS + w) for w in range(ROWS)], axis=0)
        value = (got + sig[rows, :].astype(F32)).astype(BF)
        natural = dot(back_matrix * mperm[n].astype(BF), value)
        out[pl.ds(n * ROWS, ROWS)] = natural.reshape(ROWS, TS, CH)
        return carry

    lax.fori_loop(0, TS // ROWS, convolve, 0)


def back(nb, me, recv, dconv, sig, mperm, kern):
    return pl.pallas_call(
        back_kernel,
        out_shape=jax.ShapeDtypeStruct((TS, TS, CH), F32),
        in_specs=[sspec(), sspec()] + [vspec()] * 5,
        out_specs=vspec(),
        scratch_shapes=[
            pltpu.VMEM((TS + 2 * R, NP * NS, CH), F32),
            pltpu.VMEM(((TS + 2 * R) * HG, CH), F32),
            pltpu.VMEM((49, NS, CH), F32),
        ],
        compiler_params=pltpu.CompilerParams(vmem_limit_bytes=VMEM_LIMIT),
    )(nb, me, recv, dconv, sig, mperm, kern)


ROW = 8
NCH = 17


def sum_kernel(
    n, g, gwi, gwot, small, win, wout, gain, beta, bout, scale,
    d_wi, d_wo, d_small, d_bi, d_beta, d_gain, d_scale,
    send1, recv1, send2, recv2, recv3, send4, recv4, final, ss1, rs1, ss2, rs2, ss3, rs3, ss4, rs4,
):
    me = lax.axis_index("tiles")
    groups = n // ROW
    r = lax.rem(me, ROW)
    z = me // ROW

    def row_peer(d):
        return z * ROW + lax.rem(r + d, ROW)

    def group_peer(d):
        return lax.rem(z + d, groups) * ROW + r

    barrier = pltpu.get_barrier_semaphore()
    for d in range(1, ROW):
        pl.semaphore_signal(barrier, inc=1, device_id=(row_peer(d),), device_id_type=MESH)
    for d in range(1, groups):
        pl.semaphore_signal(barrier, inc=1, device_id=(group_peer(d),), device_id_type=MESH)
    for which, ref in ((0, gwi), (1, gwot)):
        for p in range(4):
            for c in range(16):
                rb, lb = p * 4 + c // 4, c % 4
                send1[which * 4 + p, c] = ref[rb * 8 : rb * 8 + 8, lb * CH : lb * CH + CH].astype(BF)
    for p in range(ROW):
        send1[p, 16] = small[p * 8 : p * 8 + 8, :].astype(BF)
    pl.semaphore_wait(barrier, ROW - 1 + groups - 1)

    def send(src, dst, ss, rs, d, peer):
        return pltpu.make_async_remote_copy(
            src_ref=src, dst_ref=dst, send_sem=ss.at[d], recv_sem=rs.at[d],
            device_id=(peer,), device_id_type=MESH,
        )

    stage = [
        send(send1.at[lax.rem(r + d, ROW)], recv1.at[d], ss1, rs1, d, row_peer(d)) for d in range(1, ROW)
    ]
    for copy in stage:
        copy.start()
    for copy in stage:
        copy.wait()
    for c in range(NCH):
        total = send1[r, c].astype(F32)
        for d in range(1, ROW):
            total = total + recv1[d, c].astype(F32)
        if c < 16:
            send2[c, 0] = total
        else:
            for k in range(16):
                send2[k, 1] = total
    stage = [
        send(send2.at[lax.rem(z + d, groups)], recv2.at[d], ss2, rs2, d, group_peer(d))
        for d in range(1, groups)
    ]
    for copy in stage:
        copy.start()
    recv2[0] = send2[z]
    for copy in stage:
        copy.wait()
    for k in range(2):
        total = None
        for d in range(groups):
            part = recv2[lax.rem(z - d + groups, groups), k]
            total = part if total is None else total + part
        if k == 0:
            recv3[0] = total
        else:
            send4[16] = (total * g).astype(BF)
    stage = [send(recv3.at[0], recv3.at[d], ss3, rs3, d, group_peer(d)) for d in range(1, groups)]
    for copy in stage:
        copy.start()
    for copy in stage:
        copy.wait()
    for c in range(groups):
        send4[c] = (recv3[c] * g).astype(BF)
    stage = [send(send4, recv4.at[d], ss4, rs4, d, row_peer(d)) for d in range(1, ROW)]
    for copy in stage:
        copy.start()
    recv4[0] = send4[...]
    for copy in stage:
        copy.wait()
    for p in range(ROW):
        slot = lax.rem(r - p + ROW, ROW)
        for c in range(16):
            value = recv4[slot, lax.rem(z - c + groups, groups)].astype(F32)
            rb, lb = (p % 4) * 4 + c // 4, c % 4
            out = d_wi if p < 4 else final
            out[rb * 8 : rb * 8 + 8, lb * CH : lb * CH + CH] = value
        d_small[p * 8 : p * 8 + 8, :] = recv4[slot, 16].astype(F32)
    d_wo[...] = final[...].T
    ones = jnp.full((8, win.shape[1]), 1.0, BF)
    last = (((1,), (1,)), ((), ()))

    def split_dot(left, right, exact_left):
        wide = right if exact_left else left
        high = wide.astype(BF)
        low = (wide - high.astype(F32)).astype(BF)
        if exact_left:
            return lax.dot_general(left, high, last, preferred_element_type=F32) + lax.dot_general(
                left, low, last, preferred_element_type=F32
            )
        return lax.dot_general(high, right, last, preferred_element_type=F32) + lax.dot_general(
            low, right, last, preferred_element_type=F32
        )

    bias_in = jnp.concatenate([d_small[51 + w : 52 + w, :] for w in range(4)], axis=1)
    d_bi[...] = bias_in
    wi = win[...]
    row_beta = split_dot(jnp.broadcast_to(bias_in, (8, bias_in.shape[1])), wi, False)[0:1]
    row_gain = split_dot(ones, wi.astype(F32) * d_wi[...], True)[0:1]
    d_beta[...] = row_beta
    d_gain[...] = (row_gain - beta[...] * row_beta) / gain[...]
    row_scale = split_dot(ones, wout[...].astype(F32).T * final[...], True)[0:1]
    d_scale[...] = (row_scale + bout[...] * d_small[50:51, :]) / scale[...]


def sum_all(gwi, gwot, small, win, wout, gain, beta, bout, scale, n, g, cid):
    hidden = gwi.shape[1]
    groups = n // ROW
    shape = lambda *dims: jax.ShapeDtypeStruct(dims, F32)
    dma = pltpu.SemaphoreType.DMA
    return pl.pallas_call(
        functools.partial(sum_kernel, n, g),
        out_shape=(
            shape(CH, hidden), shape(hidden, CH), shape(64, CH), shape(1, hidden),
            shape(1, CH), shape(1, CH), shape(1, CH),
        ),
        in_specs=[vspec()] * 9,
        out_specs=(vspec(),) * 7,
        scratch_shapes=[
            pltpu.VMEM((ROW, NCH, 8, CH), BF),
            pltpu.VMEM((ROW, NCH, 8, CH), BF),
            pltpu.VMEM((16, 2, 8, CH), F32),
            pltpu.VMEM((16, 2, 8, CH), F32),
            pltpu.VMEM((16, 8, CH), F32),
            pltpu.VMEM((NCH, 8, CH), BF),
            pltpu.VMEM((ROW, NCH, 8, CH), BF),
            pltpu.VMEM((CH, hidden), F32),
            dma((ROW,)), dma((ROW,)), dma((groups,)), dma((groups,)),
            dma((groups,)), dma((groups,)), dma((ROW,)), dma((ROW,)),
        ],
        compiler_params=pltpu.CompilerParams(
            collective_id=cid, has_side_effects=True, vmem_limit_bytes=VMEM_LIMIT
        ),
    )(gwi, gwot, small, win, wout, gain, beta, bout, scale)


def mask_rows(mask):
    wide = ((0, 0), (0, 0), (0, CH - TS))
    mnat = jnp.pad(mask[:, None, :], wide)
    mtr = jnp.pad(mask.T[:, None, :], wide)
    mperm = mask.reshape(TS, NS, NQ).transpose(0, 2, 1).reshape(TS // ROWS, 1, BLOCK)
    return mnat, mtr, mperm


def per_device(
    fields, cotangent, ocean_mask, neighbours, kernel, conv_bias, ln_gain, ln_bias,
    weight_in, bias_in, weight_out, bias_out, layer_scale,
):
    n = lax.axis_size("tiles")
    me = lax.axis_index("tiles").astype(jnp.int32).reshape(1)
    fields, cotangent = fields[0], cotangent[0]
    mnat, mtr, mperm = mask_rows(ocean_mask[0].astype(F32))
    kern = kernel.reshape(49, 1, CH)
    row = lambda v: v.reshape(1, -1)
    gain, beta, bout, scale = row(ln_gain), row(ln_bias), row(bias_out), row(layer_scale)
    recv = exchange(pack(neighbours, me, fields, mnat, mtr), n, 0)
    updated, dconv, sig, pieces, gwi, gwot, small = core(
        neighbours, me, fields, cotangent, recv, mnat, mperm, kern, row(conv_bias), gain,
        beta, weight_in, row(bias_in), weight_out, bout, scale,
    )
    d_recv = exchange(pieces, n, 1)
    d_fields = back(neighbours, me, d_recv, dconv, sig, mperm, kern)
    g = 1.0 / math.sqrt(n * TS * TS)
    d_wi, d_wo, s, d_bi, d_beta, d_gain, d_scale = sum_all(
        gwi, gwot, small, weight_in, weight_out, gain, beta, bout, scale, n, g, 2
    )
    return (
        updated[None], d_fields[None], s[:49].reshape(7, 7, CH), s[49], d_gain[0], d_beta[0],
        d_wi, d_bi[0], d_wo, s[50], d_scale[0],
    )


def solution(mesh):
    split = P("tiles")
    whole = P()
    return jax.shard_map(
        per_device,
        mesh=mesh,
        in_specs=(split,) * 4 + (whole,) * 9,
        out_specs=(split, split) + (whole,) * 9,
        check_vma=False,
    )
```

```python
import functools
import math

import jax
import jax.numpy as jnp
from jax import lax
from jax.experimental import pallas as pl
from jax.experimental.pallas import tpu as pltpu
from jax.sharding import PartitionSpec as P

REACH = 7
OFFS = [o for o in range(-REACH, REACH + 1) if o != 0]
NOFF = len(OFFS)
EPS = 1e-06
GELU_K = 0.7978845608028654
GELU_C = 0.044715
MESH = pl.DeviceIdType.MESH
BF = jnp.bfloat16
F32 = jnp.float32
TS = 64
CH = 128
R = 3
NS = 8
NQ = 8
HG = 16
NP = NQ + 6
STRIP_OF_SIDE = (0, 1, 2, 3, 0, 0, 1, 1)
VMEM_LIMIT = 60 << 20


def vspec():
    return pl.BlockSpec(memory_space=pltpu.VMEM)


def sspec():
    return pl.BlockSpec(memory_space=pltpu.SMEM)


def strip_index(nb_ref, me, off):
    idx = jnp.int32(0)
    for side in range(8):
        idx = jnp.where(nb_ref[0, side] == me + off, STRIP_OF_SIDE[side], idx)
    return idx


def recv_slot(nb_ref, me, side):
    nb = nb_ref[0, side]
    off = nb - me
    slot = jnp.where(off < 0, off + REACH, off + REACH - 1)
    listed = nb >= 0
    slot = jnp.where(listed, jnp.clip(slot, 0, NOFF - 1), 0)
    return slot, jnp.where(listed, 1.0, 0.0).astype(F32)


def plane_matrix(permuted):
    row = lax.broadcasted_iota(jnp.int32, (NP * NS, CH), 0)
    lane = lax.broadcasted_iota(jnp.int32, (NP * NS, CH), 1)
    col = NQ * (row % NS) + row // NS - R
    inner = (col % NQ) * NS + col // NQ if permuted else col
    target = jnp.where(col < 0, TS + R + col, jnp.where(col >= TS, col + R, inner))
    return jnp.where(lane == target, 1.0, 0.0).astype(F32)


def unpermute_matrix(rows):
    n = TS * rows
    row = lax.broadcasted_iota(jnp.int32, (n, n), 0)
    lane = lax.broadcasted_iota(jnp.int32, (n, n), 1)
    col = row % TS
    target = (row // TS) * TS + (col % NQ) * NS + col // NQ
    return jnp.where(lane == target, 1.0, 0.0)


def dot(a, b):
    return jnp.dot(a, b, preferred_element_type=F32)


def write_pieces(nb_ref, me, strips, out):
    for k, off in enumerate(OFFS):
        out[k] = strips[strip_index(nb_ref, me, off)]


def pack_kernel(nb_ref, me_ref, top, bottom, left, right, mnat, mtr, out, strips, cols):
    me = me_ref[0]
    eye = jnp.where(
        lax.broadcasted_iota(jnp.int32, (TS, TS), 0) == lax.broadcasted_iota(jnp.int32, (TS, TS), 1),
        1.0,
        0.0,
    ).astype(F32)

    def masked(mask_row, value):
        return dot((eye * mask_row[:, :TS]).astype(BF), value).astype(BF)

    for w in range(R):
        strips[0, w] = masked(mnat[w], top[w])
        strips[1, w] = masked(mnat[TS - R + w], bottom[w + 1])
    for which, block, first in ((2, left, 0), (3, right, HG - R)):
        cols[...] = block[...].astype(F32).reshape(TS * HG, CH)
        for w in range(R):
            value = cols[pl.ds(first + w, TS, stride=HG), :].astype(BF)
            column = w if which == 2 else TS - R + w
            strips[which, w] = masked(mtr[column], value)
    write_pieces(nb_ref, me, strips, out)


def pack(nb, me, fields, mnat, mtr):
    n = fields.shape[0] // TS
    del n
    return pl.pallas_call(
        pack_kernel,
        grid=(1,),
        out_shape=jax.ShapeDtypeStruct((NOFF, R, TS, CH), BF),
        in_specs=[
            sspec(),
            sspec(),
            pl.BlockSpec((4, TS, CH), lambda i: (0, 0, 0)),
            pl.BlockSpec((4, TS, CH), lambda i: (TS // 4 - 1, 0, 0)),
            pl.BlockSpec((TS, HG, CH), lambda i: (0, 0, 0)),
            pl.BlockSpec((TS, HG, CH), lambda i: (0, TS // HG - 1, 0)),
            pl.BlockSpec((TS, 1, CH), lambda i: (0, 0, 0)),
            pl.BlockSpec((TS, 1, CH), lambda i: (0, 0, 0)),
        ],
        out_specs=pl.BlockSpec((NOFF, R, TS, CH), lambda i: (0, 0, 0, 0)),
        scratch_shapes=[pltpu.VMEM((4, R, TS, CH), BF), pltpu.VMEM((TS * HG, CH), F32)],
        compiler_params=pltpu.CompilerParams(vmem_limit_bytes=VMEM_LIMIT),
    )(nb, me, fields, fields, fields, fields, mnat, mtr)


def exchange_kernel(n, pieces, out, send_sem, recv_sem):
    me = lax.axis_index("tiles")
    barrier = pltpu.get_barrier_semaphore()
    for off in OFFS:
        pl.semaphore_signal(barrier, inc=1, device_id=(lax.rem(me + off + n, n),), device_id_type=MESH)
    pl.semaphore_wait(barrier, NOFF)
    copies = []
    for k, off in enumerate(OFFS):
        copies.append(
            pltpu.make_async_remote_copy(
                src_ref=pieces.at[k],
                dst_ref=out.at[NOFF - 1 - k],
                send_sem=send_sem.at[k],
                recv_sem=recv_sem.at[NOFF - 1 - k],
                device_id=(lax.rem(me + off + n, n),),
                device_id_type=MESH,
            )
        )
    order = sorted(range(NOFF), key=lambda k: -abs(OFFS[k]))
    for k in order:
        copies[k].start()
    for k in order:
        copies[k].wait()


def exchange(pieces, n, cid):
    return pl.pallas_call(
        functools.partial(exchange_kernel, n),
        out_shape=jax.ShapeDtypeStruct(pieces.shape, pieces.dtype),
        in_specs=[pl.BlockSpec(memory_space=pltpu.VMEM)],
        out_specs=pl.BlockSpec(memory_space=pltpu.VMEM),
        scratch_shapes=[pltpu.SemaphoreType.DMA((NOFF,)), pltpu.SemaphoreType.DMA((NOFF,))],
        compiler_params=pltpu.CompilerParams(
            collective_id=cid, has_side_effects=True, vmem_limit_bytes=VMEM_LIMIT
        ),
    )(pieces)


def place_halo_columns(nb_ref, me, recv, halo):
    halo[...] = jnp.zeros(halo.shape, F32)
    west, _ = recv_slot(nb_ref, me, 2)
    east, _ = recv_slot(nb_ref, me, 3)
    for w in range(R):
        halo[pl.ds(R * HG + w, TS, stride=HG), :] = recv[west, w].astype(F32)
        halo[pl.ds(R * HG + R + w, TS, stride=HG), :] = recv[east, w].astype(F32)
    for side, row0, col0 in ((4, 0, 0), (5, 0, R), (6, R + TS, 0), (7, R + TS, R)):
        slot, _ = recv_slot(nb_ref, me, side)
        first = TS - R if col0 == 0 else 0
        for w in range(R):
            at = (row0 + w) * HG + col0
            halo[at : at + R, :] = recv[slot, w].astype(F32)[first : first + R, :]


def flag_lanes(nb_ref, me, sides):
    lane = lax.broadcasted_iota(jnp.int32, (1, CH), 1)
    total = jnp.zeros((1, CH), F32)
    for side, low, high in zip(sides, (0, TS, TS + R), (TS, TS + R, TS + 2 * R)):
        if side is None:
            continue
        flag = recv_slot(nb_ref, me, side)[1]
        total = total + jnp.where((lane >= low) & (lane < high), flag, 0.0)
    return total


def fill_edge_rows(nb_ref, me, recv, halo, planes):
    matrix = plane_matrix(False)
    for sides, row0 in (((0, 4, 5), 0), ((1, 6, 7), R + TS)):
        flags = flag_lanes(nb_ref, me, sides)
        lhs = (matrix * flags).astype(BF)
        slot, _ = recv_slot(nb_ref, me, sides[0])
        for w in range(R):
            side_cols = halo[(row0 + w) * HG : (row0 + w + 1) * HG, :].astype(BF)
            rhs = jnp.concatenate([recv[slot, w], side_cols, jnp.zeros((48, CH), BF)], axis=0)
            planes[row0 + w] = dot(lhs, rhs)


def conv_row(planes, taps, i):
    acc = [None] * NQ
    for a in range(7):
        row = [planes[i + a, p * NS : (p + 1) * NS, :] for p in range(NP)]
        for b in range(7):
            tap = taps[a * 7 + b]
            for q in range(NQ):
                term = row[q + b] * tap
                acc[q] = term if acc[q] is None else acc[q] + term
    return jnp.concatenate(acc, axis=0)


def fold(value):
    return jnp.sum(value.reshape(-1, 8, value.shape[-1]), axis=0)


def load_halo(nb_ref, me, recv, side_planes, planes):
    for side, base in ((2, 0), (3, R * NS + NS - 1)):
        slot, flag = recv_slot(nb_ref, me, side)
        for w in range(R):
            side_planes[pl.ds(R * SP + base + w * NS, TS, stride=SP), :] = recv[slot, w].astype(F32) * flag
    matrix = edge_matrix()
    for sides, row0 in (((0, 4, 5), 0), ((1, 6, 7), R + TS)):
        slot, flag = recv_slot(nb_ref, me, sides[0])
        west, west_flag = recv_slot(nb_ref, me, sides[1])
        east, east_flag = recv_slot(nb_ref, me, sides[2])
        own = (matrix * flag).astype(BF)
        west_lanes = (matrix * west_flag).astype(BF)
        east_lanes = (matrix * east_flag).astype(BF)
        lane = lax.broadcasted_iota(jnp.int32, (NP * NS, CH), 1)
        lhs = jnp.where(lane < TS, own, jnp.where(lane < TS + HG, west_lanes, east_lanes))
        for w in range(R):
            lower = recv[west, w][TS - HG :]
            upper = recv[east, w][:HG]
            rhs = jnp.concatenate([recv[slot, w], lower, upper, jnp.zeros((32, CH), BF)], axis=0)
            planes[row0 + w] = dot(lhs, rhs)


ROWS = 4
BLOCK = ROWS * TS
CONTRACT0 = (((0,), (0,)), ((), ()))
ROW = 8
SP = 6 * NS


def edge_matrix():
    row = lax.broadcasted_iota(jnp.int32, (NP * NS, CH), 0)
    lane = lax.broadcasted_iota(jnp.int32, (NP * NS, CH), 1)
    col = NQ * (row % NS) + row // NS - R
    target = jnp.where(col < 0, TS + HG + col, jnp.where(col >= TS, col + HG, col))
    return jnp.where(lane == target, 1.0, 0.0).astype(F32)


def tail_kernel(
    n, nb_ref, fields, cot, recv, mnat, kern, cbias, gain, beta, win, bin_, wout, bout, scale,
    updated, value_out, sums, small_out,
    planes, halo, taps, cv, df, wit, wot, strips, gbi, gsum, dconv, sig_out, gwi, gwot, small, side_planes,
    pieces, d_recv, send1, recv1, sends, recvs, send2, recv2, sendt, recvt, recv3, send4, recv4,
    se, re, ss1, rs1, sss, rss, ss2, rs2, sst, rst, ss3, rs3, ss4, rs4,
):
    me = lax.axis_index("tiles")
    groups = n // ROW
    r = lax.rem(me, ROW)
    z = me // ROW

    def row_peer(d):
        return z * ROW + lax.rem(r + d, ROW)

    def group_peer(d):
        return lax.rem(z + d, groups) * ROW + r

    def near_peer(off):
        return lax.rem(me + off + n, n)

    barrier = pltpu.get_barrier_semaphore()
    for d in range(1, ROW):
        pl.semaphore_signal(barrier, inc=1, device_id=(row_peer(d),), device_id_type=MESH)
    for d in range(1, groups):
        pl.semaphore_signal(barrier, inc=1, device_id=(group_peer(d),), device_id_type=MESH)
    for off in OFFS:
        pl.semaphore_signal(barrier, inc=1, device_id=(near_peer(off),), device_id_type=MESH)

    def send(src, dst, ss, rs, d, peer):
        return pltpu.make_async_remote_copy(
            src_ref=src, dst_ref=dst, send_sem=ss.at[d], recv_sem=rs.at[d],
            device_id=(peer,), device_id_type=MESH,
        )

    place_halo_columns(nb_ref, me, recv, halo)
    for t in range(49):
        taps[t] = jnp.broadcast_to(kern[t], (NS, CH))
    wit[...] = win[...].T
    wot[...] = wout[...].T
    fill_edge_rows(nb_ref, me, recv, halo, planes)
    matrix = plane_matrix(False)
    flags = flag_lanes(nb_ref, me, (None, 2, 3))

    def prepare(i, carry):
        lhs = (matrix * (mnat[i] + flags)).astype(BF)
        side_cols = halo[pl.ds(pl.multiple_of((i + R) * HG, HG), HG), :].astype(BF)
        pad = jnp.zeros((48, CH), BF)
        left = jnp.concatenate([fields[i], side_cols, pad], axis=0)
        right = jnp.concatenate([cot[i], jnp.zeros((64, CH), BF)], axis=0)
        out = dot(lhs, jnp.concatenate([left, right], axis=1))
        planes[i + R] = out[:, :CH]
        sig_out[pl.ds(pl.multiple_of(i * TS, TS), TS), :] = out[R * NS : R * NS + TS, CH:].astype(BF)
        return carry

    lax.fori_loop(0, TS, prepare, 0)

    def convolve(i, carry):
        cv[pl.ds(pl.multiple_of(i * TS, TS), TS), :] = conv_row(planes, taps, i) + cbias[...]
        return carry

    lax.fori_loop(0, TS, convolve, 0)

    gwi[...] = jnp.zeros(gwi.shape, F32)
    gwot[...] = jnp.zeros(gwot.shape, F32)
    gbi[...] = jnp.zeros(gbi.shape, F32)
    gsum[...] = jnp.zeros(gsum.shape, F32)
    small[...] = jnp.zeros(small.shape, F32)
    side_planes[...] = jnp.zeros(side_planes.shape, F32)
    ones = jnp.full((CH, CH), 1.0 / CH, BF)
    all_ones = jnp.full((8, BLOCK), 1.0, BF)
    ones2 = jnp.full((2 * CH, CH), 1.0 / CH, BF)

    def block(m, carry):
        rows = pl.ds(pl.multiple_of(m * BLOCK, BLOCK), BLOCK)
        x = cv[rows, :]
        x_high = x.astype(BF)
        x_low = (x - x_high.astype(F32)).astype(BF)
        centred = x - dot(jnp.concatenate([x_high, x_low], axis=1), ones2)
        inv = lax.rsqrt(dot((centred * centred).astype(BF), ones) + EPS)
        normed = centred * inv
        lifted = (normed * gain[...] + beta[...]).astype(BF)
        sig = sig_out[rows, :].astype(F32)
        d_branch = sig * scale[...]
        branch_low = d_branch.astype(BF)
        hidden = dot(lifted, win[...]) + bin_[...]
        d_act = dot(branch_low, wot[...])
        square = hidden * hidden
        half = 0.5 * hidden
        t = jnp.tanh(hidden * (GELU_K + (GELU_K * GELU_C) * square))
        up = 1.0 + t
        act = (half * up).astype(BF)
        slope = 0.5 * up + (half * (1.0 - t * t)) * (GELU_K + (3.0 * GELU_K * GELU_C) * square)
        hidden_low = (d_act * slope).astype(BF)
        branch = dot(act, wout[...]) + bout[...]
        d_lifted = dot(hidden_low, wit[...])
        gwot[...] += lax.dot_general(branch_low, act, CONTRACT0, preferred_element_type=F32)
        gwi[...] += lax.dot_general(lifted, hidden_low, CONTRACT0, preferred_element_type=F32)
        gbi[...] += dot(all_ones, hidden_low)
        e = d_lifted * gain[...]
        en = (e * normed).astype(BF)
        d_conv = inv * (e - dot(e.astype(BF), ones) - normed * dot(en, ones))
        gsum[0] += fold(d_conv)
        gsum[1] += fold(d_branch)
        df[rows, :] = d_conv
        dconv[rows, :] = d_conv.astype(BF)
        middle = jnp.concatenate(
            [planes[m * ROWS + R + w, R * NS : R * NS + TS, :] for w in range(ROWS)], axis=0
        )
        updated[rows, :] = (middle + scale[...] * branch).astype(BF)
        return carry

    lax.fori_loop(0, TS // ROWS, block, 0)

    one_row = unpermute_matrix(1).astype(BF)
    for w in range(R):
        strips[0, w] = dot(one_row, dconv[w * TS : (w + 1) * TS, :]).astype(BF)
        low = TS - R + w
        strips[1, w] = dot(one_row, dconv[low * TS : (low + 1) * TS, :]).astype(BF)
        for which, col in ((2, w), (3, TS - R + w)):
            first = (col % NQ) * NS + col // NQ
            strips[which, w] = df[pl.ds(first, TS, stride=TS), :].astype(BF)
    write_pieces(nb_ref, me, strips, pieces)
    for which, ref in ((0, gwi), (1, gwot)):
        for p in range(4):
            for c in range(16):
                rb, lb = p * 4 + c // 4, c % 4
                send1[which * 4 + p, c] = ref[rb * 8 : rb * 8 + 8, lb * CH : lb * CH + CH].astype(BF)

    pl.semaphore_wait(barrier, ROW - 1 + groups - 1 + NOFF)
    near = []
    for k, off in enumerate(OFFS):
        near.append(
            pltpu.make_async_remote_copy(
                src_ref=pieces.at[k], dst_ref=d_recv.at[NOFF - 1 - k], send_sem=se.at[k],
                recv_sem=re.at[NOFF - 1 - k], device_id=(near_peer(off),), device_id_type=MESH,
            )
        )
    stage1 = [
        send(send1.at[lax.rem(r + d, ROW)], recv1.at[d], ss1, rs1, d, row_peer(d)) for d in range(1, ROW)
    ]
    for copy in stage1:
        copy.start()
    for k in sorted(range(NOFF), key=lambda k: -abs(OFFS[k])):
        near[k].start()

    for a in range(7):

        def gather(i, accs):
            accs = list(accs)
            row = [planes[i + a, p * NS : (p + 1) * NS, :] for p in range(NP)]
            first = pl.multiple_of(i * TS, TS)
            for q in range(NQ):
                grad = df[pl.ds(first + q * NS, NS), :]
                for b in range(7):
                    accs[b] = accs[b] + row[q + b] * grad
            return tuple(accs)

        accs = lax.fori_loop(0, TS, gather, tuple(jnp.zeros((8, CH), F32) for _ in range(7)))
        for b in range(7):
            small[a * 7 + b : a * 7 + b + 1, :] = jnp.sum(accs[b], axis=0, keepdims=True)
    small[49:50, :] = jnp.sum(gsum[0], axis=0, keepdims=True)
    small[50:51, :] = jnp.sum(gsum[1], axis=0, keepdims=True)
    for w in range(4):
        small[51 + w : 52 + w, :] = gbi[0:1, w * CH : (w + 1) * CH]
    for p in range(ROW):
        sends[p] = small[p * 8 : p * 8 + 8, :]

    for copy in stage1:
        copy.wait()
    for c in range(16):
        total = send1[r, c].astype(F32)
        for d in range(1, ROW):
            total = total + recv1[d, c].astype(F32)
        send2[c] = total
    stages = [send(sends.at[lax.rem(r + d, ROW)], recvs.at[d], sss, rss, d, row_peer(d)) for d in range(1, ROW)]
    for copy in stages:
        copy.start()
    stage2 = [
        send(send2.at[lax.rem(z + d, groups)], recv2.at[d], ss2, rs2, d, group_peer(d))
        for d in range(1, groups)
    ]
    for copy in stage2:
        copy.start()
    recv2[0] = send2[z]

    for t in range(49):
        taps[t] = jnp.broadcast_to(kern[48 - t], (NS, CH))
    for w in range(R):
        planes[w] = jnp.zeros((NP * NS, CH), F32)
        planes[R + TS + w] = jnp.zeros((NP * NS, CH), F32)
    lane = lax.broadcasted_iota(jnp.int32, (1, CH), 1)
    own = (plane_matrix(True) * jnp.where(lane < TS, 1.0, 0.0)).astype(BF)[:, :TS]

    def prepare_back(i, carry):
        planes[i + R] = dot(own, dconv[pl.ds(pl.multiple_of(i * TS, TS), TS), :])
        return carry

    lax.fori_loop(0, TS, prepare_back, 0)

    for copy in stages:
        copy.wait()
    total = sends[r]
    for d in range(1, ROW):
        total = total + recvs[d]
    sendt[...] = total
    recvt[0] = total
    staget = [send(sendt, recvt.at[d], sst, rst, d, group_peer(d)) for d in range(1, groups)]

    def convolve_back(i, carry):
        rows = pl.ds(pl.multiple_of(i * TS, TS), TS)
        cv[rows, :] = conv_row(planes, taps, i) + sig_out[rows, :].astype(F32)
        return carry

    lax.fori_loop(0, 8, convolve_back, 0)
    for copy in staget:
        copy.start()
    for copy in stage2:
        copy.wait()
    total = None
    for d in range(groups):
        part = recv2[lax.rem(z - d + groups, groups)]
        total = part if total is None else total + part
    recv3[0] = total
    stage3 = [send(recv3.at[0], recv3.at[d], ss3, rs3, d, group_peer(d)) for d in range(1, groups)]
    lax.fori_loop(8, 16, convolve_back, 0)
    for copy in stage3:
        copy.start()
    lax.fori_loop(16, 36, convolve_back, 0)
    for copy in staget:
        copy.wait()
    for copy in stage3:
        copy.wait()
    total = None
    for d in range(groups):
        part = recvt[lax.rem(z - d + groups, groups)]
        total = part if total is None else total + part
    g = 1.0 / math.sqrt(n * TS * TS)
    send4[16] = (total * g).astype(BF)
    for c in range(groups):
        send4[c] = (recv3[c] * g).astype(BF)
    recv4[0] = send4[...]
    stage4 = [send(send4, recv4.at[d], ss4, rs4, d, row_peer(d)) for d in range(1, ROW)]
    lax.fori_loop(36, 44, convolve_back, 0)
    for copy in stage4:
        copy.start()
    lax.fori_loop(44, TS, convolve_back, 0)

    for k in range(NOFF):
        near[k].wait()
    load_halo(nb_ref, me, d_recv, side_planes, planes)
    for i in (0, 1, 2, TS - 3, TS - 2, TS - 1):
        acc = [jnp.zeros((NS, CH), F32)] * NQ
        for a in range(7):
            if R <= i + a < R + TS:
                continue
            for b in range(7):
                tap = taps[a * 7 + b]
                for q in range(NQ):
                    acc[q] = acc[q] + planes[i + a, (q + b) * NS : (q + b + 1) * NS, :] * tap
        cv[i * TS : (i + 1) * TS, :] += jnp.concatenate(acc, axis=0)

    def correct(i, carry):
        acc = [None] * NQ
        for a in range(7):
            first = pl.multiple_of((i + a) * SP, SP)
            for p in range(6):
                plane = p if p < R else p - R + NQ + R
                value = side_planes[pl.ds(first + p * NS, NS), :]
                for b in range(7):
                    q = plane - b
                    if 0 <= q < NQ:
                        term = value * taps[a * 7 + b]
                        acc[q] = term if acc[q] is None else acc[q] + term
        for q in range(NQ):
            rows = pl.ds(pl.multiple_of(i * TS, TS) + q * NS, NS)
            got = cv[rows, :]
            cv[rows, :] = got if acc[q] is None else got + acc[q]
        return carry

    lax.fori_loop(0, TS, correct, 0)
    value_out[...] = cv[...].astype(BF)

    for copy in stage4:
        copy.wait()
    for p in range(ROW):
        slot = lax.rem(r - p + ROW, ROW)
        for c in range(16):
            value = recv4[slot, lax.rem(z - c + groups, groups)].astype(F32)
            rb, lb = (p % 4) * 4 + c // 4, c % 4
            sums[p // 4, rb * 8 : rb * 8 + 8, lb * CH : lb * CH + CH] = value
        small_out[p * 8 : p * 8 + 8, :] = recv4[slot, 16].astype(F32)


def tail(nb, fields, cot, recv, mnat, kern, cbias, gain, beta, win, bin_, wout, bout, scale, n, cid):
    hidden = win.shape[1]
    groups = n // ROW
    dma = pltpu.SemaphoreType.DMA
    f = lambda *dims: pltpu.VMEM(dims, F32)
    h = lambda *dims: pltpu.VMEM(dims, BF)
    return pl.pallas_call(
        functools.partial(tail_kernel, n),
        out_shape=(
            jax.ShapeDtypeStruct((TS * TS, CH), BF),
            jax.ShapeDtypeStruct((TS * TS, CH), BF),
            jax.ShapeDtypeStruct((2, CH, hidden), F32),
            jax.ShapeDtypeStruct((64, CH), F32),
        ),
        in_specs=[sspec()] + [vspec()] * 13,
        out_specs=(vspec(),) * 4,
        scratch_shapes=[
            f(TS + 2 * R, NP * NS, CH), f((TS + 2 * R) * HG, CH), f(49, NS, CH), f(TS * TS, CH),
            f(TS * TS, CH), h(hidden, CH), h(CH, hidden), h(4, R, TS, CH), f(8, hidden), f(2, 8, CH),
            h(TS * TS, CH), h(TS * TS, CH), f(CH, hidden), f(CH, hidden), f(64, CH),
            f((TS + 2 * R) * SP, CH),
            h(NOFF, R, TS, CH), h(NOFF, R, TS, CH), h(ROW, 16, 8, CH), h(ROW, 16, 8, CH),
            f(ROW, 8, CH), f(ROW, 8, CH), f(16, 8, CH), f(16, 8, CH), f(8, CH), f(16, 8, CH), f(16, 8, CH),
            h(17, 8, CH), h(ROW, 17, 8, CH),
            dma((NOFF,)), dma((NOFF,)), dma((ROW,)), dma((ROW,)), dma((ROW,)), dma((ROW,)),
            dma((groups,)), dma((groups,)), dma((groups,)), dma((groups,)), dma((groups,)), dma((groups,)),
            dma((ROW,)), dma((ROW,)),
        ],
        compiler_params=pltpu.CompilerParams(
            collective_id=cid, has_side_effects=True, vmem_limit_bytes=VMEM_LIMIT
        ),
    )(nb, fields, cot, recv, mnat, kern, cbias, gain, beta, win, bin_, wout, bout, scale)


def finish_kernel(
    up, val, mperm, sums, small, win, wout, gain, beta, bout, scale,
    updated, d_fields, d_kern, d_cb, d_bo, d_wi, d_wo, d_bi, d_beta, d_gain, d_scale,
):
    back_matrix = unpermute_matrix(ROWS).astype(BF) * mperm[0].astype(BF)
    both = dot(back_matrix, jnp.concatenate([up[...], val[...]], axis=1))
    updated[...] = both[:, :CH].astype(BF).reshape(ROWS, TS, CH)
    d_fields[...] = both[:, CH:].reshape(ROWS, TS, CH)

    @pl.when(pl.program_id(0) == 0)
    def _():
        d_wi[...] = sums[0]
        d_wo[...] = sums[1].T
        for a in range(7):
            d_kern[a] = small[a * 7 : a * 7 + 7, :]
        d_cb[...] = small[49:50, :]
        d_bo[...] = small[50:51, :]
        ones = jnp.full((8, win.shape[1]), 1.0, BF)
        last = (((1,), (1,)), ((), ()))

        def row_dot(left, right):
            return lax.dot_general(left, right, last, preferred_element_type=F32)

        def split(value):
            high = value.astype(BF)
            return high, (value - high.astype(F32)).astype(BF)

        bias_in = jnp.concatenate([small[51 + w : 52 + w, :] for w in range(4)], axis=1)
        d_bi[...] = bias_in
        wi = win[...]
        high, low = split(jnp.broadcast_to(bias_in, (8, bias_in.shape[1])))
        row_beta = (row_dot(high, wi) + row_dot(low, wi))[0:1]
        high, low = split(wi.astype(F32) * sums[0])
        row_gain = (row_dot(ones, high) + row_dot(ones, low))[0:1]
        d_beta[...] = row_beta
        d_gain[...] = (row_gain - beta[...] * row_beta) / gain[...]
        high, low = split(wout[...].astype(F32).T * sums[1])
        row_scale = (row_dot(ones, high) + row_dot(ones, low))[0:1]
        d_scale[...] = (row_scale + bout[...] * small[50:51, :]) / scale[...]


def finish(up, val, mperm, sums, small, win, wout, gain, beta, bout, scale):
    hidden = win.shape[1]
    const = lambda *dims: pl.BlockSpec(dims, lambda i: (0,) * len(dims))
    shape = lambda *dims: jax.ShapeDtypeStruct(dims, F32)
    tiles = pl.BlockSpec((ROWS, TS, CH), lambda i: (i, 0, 0))
    flat = pl.BlockSpec((BLOCK, CH), lambda i: (i, 0))
    return pl.pallas_call(
        finish_kernel,
        grid=(TS // ROWS,),
        out_shape=(
            jax.ShapeDtypeStruct((TS, TS, CH), BF), shape(TS, TS, CH), shape(7, 7, CH), shape(1, CH),
            shape(1, CH), shape(CH, hidden), shape(hidden, CH), shape(1, hidden), shape(1, CH),
            shape(1, CH), shape(1, CH),
        ),
        in_specs=[
            flat, flat, pl.BlockSpec((1, 1, BLOCK), lambda i: (i, 0, 0)), const(2, CH, hidden),
            const(64, CH), const(CH, hidden), const(hidden, CH), const(1, CH), const(1, CH),
            const(1, CH), const(1, CH),
        ],
        out_specs=(
            tiles, tiles, const(7, 7, CH), const(1, CH), const(1, CH), const(CH, hidden),
            const(hidden, CH), const(1, hidden), const(1, CH), const(1, CH), const(1, CH),
        ),
        compiler_params=pltpu.CompilerParams(vmem_limit_bytes=VMEM_LIMIT),
    )(up, val, mperm, sums, small, win, wout, gain, beta, bout, scale)


def mask_rows(mask):
    wide = ((0, 0), (0, 0), (0, CH - TS))
    mnat = jnp.pad(mask[:, None, :], wide)
    mtr = jnp.pad(mask.T[:, None, :], wide)
    mperm = mask.reshape(TS, NS, NQ).transpose(0, 2, 1).reshape(TS // ROWS, 1, BLOCK)
    return mnat, mtr, mperm


def per_device(
    fields, cotangent, ocean_mask, neighbours, kernel, conv_bias, ln_gain, ln_bias,
    weight_in, bias_in, weight_out, bias_out, layer_scale,
):
    n = lax.axis_size("tiles")
    me = lax.axis_index("tiles").astype(jnp.int32).reshape(1)
    fields, cotangent = fields[0], cotangent[0]
    mnat, mtr, mperm = mask_rows(ocean_mask[0].astype(F32))
    kern = kernel.reshape(49, 1, CH)
    row = lambda v: v.reshape(1, -1)
    gain, beta, bout, scale = row(ln_gain), row(ln_bias), row(bias_out), row(layer_scale)
    recv = exchange(pack(neighbours, me, fields, mnat, mtr), n, 0)
    up, val, sums, small = tail(
        neighbours, fields, cotangent, recv, mnat, kern, row(conv_bias), gain, beta, weight_in,
        row(bias_in), weight_out, bout, scale, n, 1,
    )
    updated, d_fields, d_kern, d_cb, d_bo, d_wi, d_wo, d_bi, d_beta, d_gain, d_scale = finish(
        up, val, mperm, sums, small, weight_in, weight_out, gain, beta, bout, scale
    )
    return (
        updated[None], d_fields[None], d_kern, d_cb[0], d_gain[0], d_beta[0], d_wi, d_bi[0], d_wo,
        d_bo[0], d_scale[0],
    )


def solution(mesh):
    split = P("tiles")
    whole = P()
    return jax.shard_map(
        per_device,
        mesh=mesh,
        in_specs=(split,) * 4 + (whole,) * 9,
        out_specs=(split, split) + (whole,) * 9,
        check_vma=False,
    )
```
